128 devices in a mesh: seq: 32 (over y, x, core), head: 4 (over z).
Axes of the slice: x: 4, y: 4, z: 4, core: 2. Of those that a mesh axis runs over, the one named last changes fastest.
Arguments:
- hidden_in: bfloat16 [8192, 2880], P(('seq', 'head')), may hold values from -16 to 16
- qkv_new: bfloat16 [8192, 8, 640], P(('seq', 'head')), may hold values from -250 to 250
- kv_cache: bfloat16 [32, 8192, 8, 128], P('seq', None, 'head'), may hold values from -4 to 4
- cache_len: int32 [32], P('seq'), may hold values from 2048 to 8192, as said below
- o_weight: bfloat16 [4096, 2880], P('head'), may hold values from -1 to 1
- norm_gain: float32 [2880], replicated, may hold values from 0.1 to 1.9
- expert_ids: int32 [8192, 4], P(('seq', 'head')), may hold values from 0 to 31, all different within a row; in each aligned block of 64 rows (0 to 63, 64 to 127, ...) at most 10 rows name the same one
- gate_weights: float32 [8192, 4], P(('seq', 'head')), may hold values from 0.1 to 1
- w_gate_up: bfloat16 [32, 2880, 2, 2880], P('seq', None, None, 'head'), may hold values from -0.109375 to 0.109375
- w_down: bfloat16 [32, 2880, 2880], P('seq', 'head'), may hold values from -0.109375 to 0.109375
Outputs:
- attn_proj: bfloat16 [8192, 2880], P(('seq', 'head'))
- moe_out: bfloat16 [8192, 2880], P(('seq', 'head'))
The draws below stay inside these ranges and needn't reach their ends.
Inputs may be any that keep to these rules, and one draw needn't show every extreme that they name: `cache_len`: some sequence has exactly 8192 live cached positions in every draw. `expert_ids`: each token names 4 different experts. Among the tokens of one device (aligned blocks of 64 tokens) no expert is named more than 10 times, a bound that some block reaches.
All inputs are finite; a program needn't handle non-finite values.
Results may differ from the reference program's by a relative error of at most 0.024.
Values may be sent and summed in bfloat16 or wider, within the bound.
A program may use at most 256 MiB of HBM per device.

```python
import math
import jax
import jax.numpy as jnp
import numpy as np
from jax import lax

D = 2880
HD = 64
KVH = 8
GQA = 8
FF = 2880
TOP = 4
NEW_TOK = 256
CACHE = 8192
SEQS = 32
TOKENS = 8192
TOK_DEV = 64
EXPERTS = 32
CAP = 10
N_HEAD = 4
DEVICES = 128


def draw_hidden_in(key, part):
    first, second = jax.random.split(key, 2)
    base = jax.random.truncated_normal(first, -4.0, 4.0, (TOKENS, D), jnp.float32)
    scales = jnp.exp(jax.random.uniform(second, (TOKENS, 1), jnp.float32, math.log(0.3), math.log(3.0)))
    return (base * scales).astype(jnp.bfloat16)


def draw_qkv_new(key, part):
    first = jax.random.fold_in(key, 0)
    base = jax.random.truncated_normal(first, -4.0, 4.0, (TOKENS, KVH, (GQA + 2) * HD), jnp.float32)
    query_part = base[:, :, :GQA * HD] * 2.0
    key_part = base[:, :, GQA * HD:(GQA + 1) * HD]
    value_part = base[:, :, (GQA + 1) * HD:]
    return jnp.concatenate([query_part, key_part, value_part], axis=2).astype(jnp.bfloat16)


def draw_cache_len(key, part):
    first, second = jax.random.split(key)
    lengths = jax.random.randint(first, (SEQS,), CACHE // 4, CACHE + 1, jnp.int32)
    chosen = jax.random.randint(second, (), 0, SEQS, jnp.int32)
    return jnp.where(jnp.arange(SEQS, dtype=jnp.int32) == chosen, CACHE, lengths).astype(jnp.int32)


def levels(stream_key, dims, cuts, low, largest):
    level = 1.0
    for axis_at, parts in cuts:
        heights = jax.random.uniform(jax.random.fold_in(jax.random.fold_in(stream_key, 6), axis_at), (parts,), jnp.float32, low / len(cuts), largest / len(cuts))
        level = level * jnp.repeat(jnp.exp(heights), dims[axis_at] // parts).reshape((-1,) + (1,) * (len(dims) - 1 - axis_at))
    return level


def deal_out(own_key, own, number, rows, count, top, most, slope):
    order = jax.random.permutation(own_key, count)
    packed, ordinary = load_shares(count, rows * top, most, slope, True), load_shares(count, rows * top, most, slope, False)
    places = jnp.arange(count)

    def named(sizes, rotation):
        used = int((sizes > 0).sum())
        fixed = max(1, used // 4)
        shifted = fixed + (places - fixed + rotation * (used - fixed)) % max(1, count - fixed)
        return jnp.zeros((count,), jnp.int32).at[order[jnp.where(places < fixed, places, shifted)]].set(jnp.asarray(sizes, jnp.int32))

    sizes = jnp.where(number % 4 == 0, named(packed, number // 4), named(ordinary, number - number // 4 - 1))
    mixed = jax.random.permutation(jax.random.fold_in(own, 3), count)
    source_of, sink = mixed[0:count // 2 * 2:2], mixed[1:count // 2 * 2:2]
    margin = jnp.minimum(sizes[source_of] - 1, most - sizes[sink]) // 2
    margin = jnp.where((source_of == order[0]) | (sink == order[0]) | (sizes[sink] == 0), 0, jnp.maximum(margin, 0))
    shifted = jax.random.randint(jax.random.fold_in(own, 4), (count // 2,), 0, 1 << 20) % (margin + 1)
    sizes = sizes.at[source_of].add(-shifted).at[sink].add(shifted)
    labels = jnp.searchsorted(jnp.cumsum(sizes), jnp.arange(rows * top), side="right").astype(jnp.int32)
    table = labels.reshape(top, rows).T
    table = table[jax.random.permutation(jax.random.fold_in(own, 1), rows)]
    rotation = jax.random.randint(jax.random.fold_in(own, 2), (rows, 1), 0, top)
    return jnp.take_along_axis(table, (jnp.arange(top)[None, :] + rotation) % top, axis=1)


def load_shares(amount, total, reach, lean, full):
    loads = [(1 << 20) // math.isqrt(rank ** lean) + 1 for rank in range(1, amount + 1)]
    largest = reach if full else min(reach, max(-(-total // amount), total * loads[0] // sum(loads)))
    least = 1 if total - largest >= amount - 1 else 0
    given, spare = [largest] + [least] * (amount - 1), total - largest - least * (amount - 1)
    while spare > 0:
        movable = [i for i in range(1, amount) if given[i] < largest] or [i for i in range(1, amount) if given[i] < reach]
        pool, remaining = sum([loads[i] for i in movable]), spare
        for i in movable:
            addition = min(reach - given[i], max(1, remaining * loads[i] // pool), spare)
            given[i] = given[i] + addition
            spare = spare - addition
    return np.array(given)


def gaussian(own_key, shape, deviation, limit, cuts=(), kind=jnp.bfloat16):
    loudness = levels(own_key, shape, cuts, -0.22, 0.18) if cuts else 1.0
    entries = jax.random.normal(own_key, shape, jnp.float32) * deviation * loudness
    return jnp.minimum(jnp.maximum(entries, -limit), limit).astype(kind)


def setup_inputs(seed: int = 0) -> dict:
    arg_keys = jax.random.split(jax.random.key(seed), 11)
    hidden_in = draw_hidden_in(jax.random.fold_in(arg_keys[10], 71), 0)
    qkv_new = draw_qkv_new(jax.random.fold_in(arg_keys[10], 71), 0)
    kv_cache = gaussian(arg_keys[2], (SEQS, CACHE, KVH, 2 * HD), 1.0, 4.0, ((0, 32), (2, 4)))
    cache_len = draw_cache_len(jax.random.fold_in(arg_keys[10], 71), 0)
    o_weight = gaussian(arg_keys[4], (KVH * GQA * HD, D), 0.2, 1.0, ((0, 4),))
    norm_gain = jnp.clip(1.0 + 0.18 * jax.random.normal(arg_keys[5], (D,), jnp.float32), 0.1, 1.9)
    expert_ids_keys = jax.random.split(jax.random.fold_in(arg_keys[6], 1), TOKENS // TOK_DEV)
    expert_ids_turns = jax.random.permutation(jax.random.fold_in(arg_keys[6], 3), TOKENS // TOK_DEV)
    expert_ids = jax.vmap(lambda own, number: deal_out(jax.random.fold_in(arg_keys[6], 2), own, number, TOK_DEV, EXPERTS, TOP, CAP, 2))(expert_ids_keys, expert_ids_turns).reshape((TOKENS, TOP))
    gate_weights = jnp.clip(0.1 + 0.9 * jax.random.uniform(arg_keys[7], (TOKENS, TOP), jnp.float32) ** levels(arg_keys[7], (TOKENS, TOP), ((0, 128),), -0.2, 0.2), 0.1, 1.0)
    w_gate_up = gaussian(arg_keys[8], (EXPERTS, D, 2, FF), D ** -0.5, 0.109375, ((0, 32), (3, 4)))
    w_down = gaussian(arg_keys[9], (EXPERTS, FF, D), FF ** -0.5, 0.109375, ((0, 32), (1, 4)))
    return dict(hidden_in=hidden_in, qkv_new=qkv_new, kv_cache=kv_cache, cache_len=cache_len, o_weight=o_weight, norm_gain=norm_gain, expert_ids=expert_ids, gate_weights=gate_weights, w_gate_up=w_gate_up, w_down=w_down)


epsilon = 1e-05

def attend(fresh_group, stored, live_len):
    fresh_len = fresh_group.shape[0]
    cached = stored.shape[0]
    head_dim = stored.shape[1] // 2
    group_size = fresh_group.shape[1] // head_dim - 2
    queries = fresh_group[:, :group_size * head_dim].reshape(fresh_len * group_size, head_dim)
    key_rows = jnp.concatenate([stored[:, :head_dim], fresh_group[:, group_size * head_dim:(group_size + 1) * head_dim]], axis=0)
    value_rows = jnp.concatenate([stored[:, head_dim:], fresh_group[:, (group_size + 1) * head_dim:]], axis=0)
    scores = jnp.einsum('qd,kd->qk', queries.astype(jnp.float32), key_rows.astype(jnp.float32)) * head_dim ** (-0.5)
    positions = lax.broadcasted_iota(jnp.int32, scores.shape, 1)
    token_pos = lax.broadcasted_iota(jnp.int32, scores.shape, 0) // group_size
    visible = (positions < live_len) | (positions >= cached) & (positions - cached <= token_pos)
    masked = jnp.where(visible, scores, -jnp.inf)
    row_max = lax.optimization_barrier(jnp.max(masked, axis=1, keepdims=True))
    exponent = jnp.where(visible, jnp.exp(masked - row_max), 0.0)
    weights = (exponent / lax.optimization_barrier(jnp.sum(exponent, axis=1, keepdims=True))).astype(jnp.bfloat16)
    result = jnp.dot(weights, value_rows, preferred_element_type=jnp.float32).astype(jnp.bfloat16)
    return result.reshape(fresh_len, group_size * head_dim)

def slot_numbers(expert_ids):
    flat_ids = expert_ids.reshape(-1, TOK_DEV * TOP)
    onehot = (flat_ids[:, :, None] == jnp.arange(EXPERTS, dtype=jnp.int32)[None, None, :]).astype(jnp.int32)
    before = jnp.cumsum(onehot, axis=1) - onehot
    return lax.optimization_barrier(jnp.sum(before * onehot, axis=2)).reshape(TOKENS, TOP).astype(jnp.int32)

def reference(hidden_in, qkv_new, kv_cache, cache_len, o_weight, norm_gain, expert_ids, gate_weights, w_gate_up, w_down):
    sequences = qkv_new.reshape(SEQS, NEW_TOK, KVH, (GQA + 2) * HD)

    def per_seq(seq_index):
        group_rows = lax.dynamic_index_in_dim(sequences, seq_index, 0, keepdims=False)
        stored_all = lax.dynamic_index_in_dim(kv_cache, seq_index, 0, keepdims=False)
        live_len = lax.dynamic_index_in_dim(cache_len, seq_index, 0, keepdims=False)

        def per_head(head_index):
            fresh_group = lax.dynamic_index_in_dim(group_rows, head_index, 1, keepdims=False)
            stored = lax.dynamic_index_in_dim(stored_all, head_index, 1, keepdims=False)
            return attend(fresh_group, stored, live_len)
        return lax.map(per_head, jnp.arange(KVH, dtype=jnp.int32))
    heads_out = lax.map(per_seq, jnp.arange(SEQS, dtype=jnp.int32))
    attention = jnp.transpose(heads_out, (0, 2, 1, 3)).reshape(TOKENS, KVH * GQA * HD)
    attn_proj = jnp.dot(attention, o_weight, preferred_element_type=jnp.float32).astype(jnp.bfloat16)
    kept_proj = lax.optimization_barrier(attn_proj)
    residual = (hidden_in.astype(jnp.float32) + kept_proj.astype(jnp.float32)).astype(jnp.bfloat16)
    widened = lax.optimization_barrier(residual).astype(jnp.float32)
    normed = (widened * lax.rsqrt(lax.optimization_barrier(jnp.mean(widened * widened, axis=1, keepdims=True)) + epsilon) * norm_gain).astype(jnp.bfloat16)
    slot_ids = slot_numbers(expert_ids)
    blocks = (jnp.arange(TOKENS, dtype=jnp.int32) // TOK_DEV)[:, None]
    dest_rows = (blocks * CAP + slot_ids).astype(jnp.int32)
    buffer = jnp.zeros((EXPERTS, DEVICES * CAP, D), jnp.bfloat16)
    buffer = buffer.at[expert_ids, dest_rows].set(jnp.broadcast_to(normed[:, None, :], (TOKENS, TOP, D)))

    def per_expert(operands):
        slot_rows, pair_weight, down_weight = operands
        gate_up = jnp.dot(slot_rows, pair_weight.reshape(D, 2 * FF), preferred_element_type=jnp.float32)
        hidden = (jax.nn.silu(gate_up[:, :FF]) * gate_up[:, FF:]).astype(jnp.bfloat16)
        pieces = jnp.einsum('rqf,qfd->qrd', hidden.reshape(-1, N_HEAD, FF // N_HEAD).astype(jnp.float32), down_weight.reshape(N_HEAD, FF // N_HEAD, D).astype(jnp.float32))
        rounded = lax.optimization_barrier(pieces.astype(jnp.bfloat16)).astype(jnp.float32)
        return lax.optimization_barrier(jnp.sum(rounded, axis=0)).astype(jnp.bfloat16)
    expert_out = lax.map(per_expert, (buffer, w_gate_up, w_down))
    picked = expert_out[expert_ids, dest_rows].astype(jnp.float32)
    moe_out = lax.optimization_barrier(jnp.sum(picked * gate_weights[:, :, None], axis=1)).astype(jnp.bfloat16)
    return (attn_proj, moe_out)
```

```python
import functools
import jax
import jax.numpy as jnp
from jax import lax
from jax.experimental import pallas as pl
from jax.experimental.pallas import tpu as pltpu
from jax.sharding import PartitionSpec as P

TOP = 4
EPS = 1e-05
LOG2E = 1.4426950408889634
MASKED = -1e30
NT = (((1,), (1,)), ((), ()))


def attend_kernel(len_ref, new_ref, kk_ref, vv_ref, out_ref, q_s, nk_s, nv_s, s_s, acc_s, *, tile):
    src_count, _, tok, width = new_ref.shape
    cached = kk_ref.shape[1]
    head_dim = kk_ref.shape[2] // 2
    group = width // head_dim - 2
    rows = group * tok
    new_len = src_count * tok
    chunk = pl.program_id(1)
    live = len_ref[0]
    factor = LOG2E * head_dim ** (-0.5)
    for r in range(group):
        wide = new_ref[chunk, 0, :, r * head_dim : (r + 1) * head_dim].astype(jnp.float32) * factor
        high = wide.astype(jnp.bfloat16)
        low = (wide - high.astype(jnp.float32)).astype(jnp.bfloat16)
        q_s[r * tok : (r + 1) * tok, :] = jnp.concatenate([high, low], axis=1)
    for s in range(src_count):
        k = new_ref[s, 0, :, group * head_dim : (group + 1) * head_dim]
        v = new_ref[s, 0, :, (group + 1) * head_dim :]
        nk_s[s * tok : (s + 1) * tok, :] = jnp.concatenate([k, k], axis=1)
        nv_s[s * tok : (s + 1) * tok, :] = jnp.concatenate([jnp.ones_like(v), v], axis=1)
    tiles = rows // tile

    def scores(i, slot):
        start = pl.multiple_of(i * tile, tile)
        q = q_s[pl.ds(start, tile), :]
        s_s[slot, :, :cached] = lax.dot_general(
            q, kk_ref[0], NT, preferred_element_type=jnp.float32
        )
        fresh = lax.dot_general(q, nk_s[...], NT, preferred_element_type=jnp.float32)
        key_pos = lax.broadcasted_iota(jnp.int32, (tile, new_len), 1)
        tok_pos = chunk * tok + (lax.broadcasted_iota(jnp.int32, (tile, new_len), 0) + start) % tok
        s_s[slot, :, cached:] = jnp.where(key_pos <= tok_pos, fresh, MASKED)

        def hide(c, carry):
            at = pl.multiple_of(c * 128, 128)
            pos = at + lax.broadcasted_iota(jnp.int32, (tile, 128), 1)
            s_s[slot, :, pl.ds(at, 128)] = jnp.where(
                pos < live, s_s[slot, :, pl.ds(at, 128)], MASKED
            )
            return carry

        lax.fori_loop(live // 128, cached // 128, hide, 0)

    def weigh(i, slot):
        start = pl.multiple_of(i * tile, tile)
        s = s_s[slot]
        p = jnp.exp2(s - jnp.max(s, axis=1, keepdims=True)).astype(jnp.bfloat16)
        acc_s[pl.ds(start, tile), :] = jnp.dot(
            p[:, :cached], vv_ref[0], preferred_element_type=jnp.float32
        ) + jnp.dot(p[:, cached:], nv_s[...], preferred_element_type=jnp.float32)

    scores(0, 0)

    def pair(u, carry):
        scores(2 * u + 1, 1)
        weigh(2 * u, 0)
        scores(lax.rem(2 * u + 2, tiles), 0)
        weigh(2 * u + 1, 1)
        return carry

    lax.fori_loop(0, tiles // 2, pair, 0)
    for r in range(group):
        acc = acc_s[r * tok : (r + 1) * tok, :]
        out_ref[:, r * head_dim : (r + 1) * head_dim] = (
            acc[:, head_dim:] / acc[:, :head_dim]
        ).astype(jnp.bfloat16)


def attention_of(fresh, kk, vv, live, tile=256):
    src_count, kv_local, tok, width = fresh.shape
    cached, lanes = kk.shape[1:]
    group = width * 2 // lanes - 2
    rows = group * tok
    return pl.pallas_call(
        functools.partial(attend_kernel, tile=tile),
        grid_spec=pltpu.PrefetchScalarGridSpec(
            num_scalar_prefetch=1,
            grid=(kv_local, src_count),
            in_specs=[
                pl.BlockSpec((src_count, 1, tok, width), lambda h, j, n: (0, h, 0, 0)),
                pl.BlockSpec((1, cached, lanes), lambda h, j, n: (h, 0, 0)),
                pl.BlockSpec((1, cached, lanes), lambda h, j, n: (h, 0, 0)),
            ],
            out_specs=pl.BlockSpec((tok, group * lanes // 2), lambda h, j, n: (j, h)),
            scratch_shapes=[
                pltpu.VMEM((rows, lanes), jnp.bfloat16),
                pltpu.VMEM((src_count * tok, lanes), jnp.bfloat16),
                pltpu.VMEM((src_count * tok, lanes), jnp.bfloat16),
                pltpu.VMEM((2, tile, cached + src_count * tok), jnp.float32),
                pltpu.VMEM((rows, lanes), jnp.float32),
            ],
        ),
        out_shape=jax.ShapeDtypeStruct(
            (src_count * tok, kv_local * group * lanes // 2), jnp.bfloat16
        ),
        compiler_params=pltpu.CompilerParams(vmem_limit_bytes=56 << 20),
    )(live, fresh, kk, vv)


def per_device(
    hidden_in,
    qkv_new,
    kv_cache,
    cache_len,
    o_weight,
    norm_gain,
    expert_ids,
    gate_weights,
    w_gate_up,
    w_down,
):
    seq_count = lax.axis_size("seq")
    head_count = lax.axis_size("head")
    tok_rows, model_width = hidden_in.shape
    experts = seq_count
    capacity = max(2, tok_rows * TOP * 5 // (4 * experts))
    half = w_gate_up.shape[3]
    head_dim = kv_cache.shape[3] // 2

    fresh = lax.all_to_all(
        jnp.transpose(qkv_new, (1, 0, 2)), "head", split_axis=0, concat_axis=0, tiled=True
    )
    fresh = fresh.reshape(head_count, -1, tok_rows, qkv_new.shape[2])
    stored = jnp.transpose(kv_cache[0], (1, 0, 2))
    k, v = stored[..., :head_dim], stored[..., head_dim:]
    kk = jnp.concatenate([k, k], axis=-1)
    vv = jnp.concatenate([jnp.ones_like(v), v], axis=-1)
    attention = attention_of(fresh, kk, vv, cache_len)
    projected = lax.psum_scatter(
        jnp.dot(attention, o_weight, preferred_element_type=jnp.float32).astype(jnp.bfloat16),
        "head",
        scatter_dimension=0,
        tiled=True,
    )
    attn_proj = projected.astype(jnp.bfloat16)
    widened = (
        (hidden_in.astype(jnp.float32) + attn_proj.astype(jnp.float32))
        .astype(jnp.bfloat16)
        .astype(jnp.float32)
    )
    normed = (
        widened
        * lax.rsqrt(jnp.mean(widened * widened, axis=1, keepdims=True) + EPS)
        * norm_gain
    ).astype(jnp.bfloat16)

    flat_ids = expert_ids.reshape(-1)
    onehot = (flat_ids[:, None] == jnp.arange(experts, dtype=jnp.int32)[None, :]).astype(jnp.int32)
    before = jnp.cumsum(onehot, axis=0) - onehot
    slot_ids = jnp.sum(before * onehot, axis=1)
    target = flat_ids * capacity + slot_ids
    places = target[None, :] == jnp.arange(experts * capacity, dtype=jnp.int32)[:, None]
    places = places.reshape(experts * capacity, tok_rows, TOP)
    gates = jnp.sum(jnp.where(places, gate_weights[None], 0.0), axis=2).T
    gates_high = gates.astype(jnp.bfloat16)
    gates_low = (gates - gates_high.astype(jnp.float32)).astype(jnp.bfloat16)
    gates = jnp.concatenate([gates_high, gates_low], axis=0)
    places = jnp.any(places, axis=2).astype(jnp.bfloat16)

    outgoing = jnp.dot(places, normed, preferred_element_type=jnp.float32).astype(jnp.bfloat16)
    outgoing = outgoing.reshape(experts, capacity, model_width)
    arrived = lax.all_to_all(outgoing, "seq", split_axis=0, concat_axis=0, tiled=True)
    rows = lax.all_gather(
        arrived.reshape(experts * capacity, model_width), "head", axis=0, tiled=True
    )
    gate_up = jnp.dot(
        rows,
        w_gate_up[0].reshape(model_width, 2 * half),
        preferred_element_type=jnp.float32,
    )
    hidden = (jax.nn.silu(gate_up[:, :half]) * gate_up[:, half:]).astype(jnp.bfloat16)
    piece = jnp.dot(hidden, w_down[0], preferred_element_type=jnp.float32).astype(jnp.bfloat16)
    summed = lax.psum_scatter(piece, "head", scatter_dimension=0, tiled=True)
    returned = lax.all_to_all(
        summed.reshape(experts, capacity, model_width), "seq", split_axis=0, concat_axis=0, tiled=True
    ).reshape(experts * capacity, model_width)
    both = jnp.dot(gates, returned, preferred_element_type=jnp.float32)
    moe_out = (both[:tok_rows] + both[tok_rows:]).astype(jnp.bfloat16)
    return (attn_proj, moe_out)


def solution(mesh):
    return jax.shard_map(
        per_device,
        mesh=mesh,
        in_specs=(
            P(("seq", "head"), None),
            P(("seq", "head"), None, None),
            P("seq", None, "head", None),
            P("seq"),
            P("head", None),
            P(),
            P(("seq", "head"), None),
            P(("seq", "head"), None),
            P("seq", None, None, "head"),
            P("seq", "head", None),
        ),
        out_specs=(P(("seq", "head"), None), P(("seq", "head"), None)),
        check_vma=False,
    )
```
